32 devices in a mesh: row: 16 (over z, x, core), col: 2 (over y).
Axes of the slice: x: 2, y: 2, z: 4, core: 2. Of those that a mesh axis runs over, the one named last changes fastest.
Arguments:
- counts: float32 [8192, 8192], P('row', 'col'), may hold values from 0 to 12, as said below
- loadings: float32 [8192, 64], P(('col', 'row')), may hold values from 0.02 to 0.4
Outputs:
- row_grad: float32 [8192, 64], P(('row', 'col'))
- col_grad: float32 [8192, 64], P(('col', 'row'))
The draws below stay inside these ranges and needn't reach their ends.
Inputs may be any that keep to these rules, and one draw needn't show every extreme that they name: `counts`: whole numbers, more of them near the diagonal.
All inputs are finite; a program needn't handle non-finite values.
Results may differ from the reference program's by a relative error of at most 0.0003.
Values sent between devices are 32-bit elements; how exact they have to be, the bound alone decides.
A program may use at most 64 MiB of HBM per device.

```python
import math
import jax
import jax.numpy as jnp
from jax import lax

RANK = 64
ROWS_DEV = 512
NBINS = 8192


def draw_counts(key, part):
    first = jnp.arange(NBINS).astype(jnp.int32)
    distance = jnp.abs(first[:, None] - first[None, :])
    ceiling = 4 + 9 // (1 + distance // 64)
    values = jax.random.randint(jax.random.fold_in(key, 11), (NBINS, NBINS), 0, 1 << 20)
    return (values % ceiling).astype(jnp.float32)


def block_scale(stream_key, extent, cuts, smallest, top_value):
    def one(position, shards_of):
        steps = jax.random.uniform(jax.random.fold_in(jax.random.fold_in(stream_key, 6), position), (shards_of,), jnp.float32, smallest / len(cuts), top_value / len(cuts))
        return jnp.repeat(jnp.exp(steps), extent[position] // shards_of).reshape((-1,) + (1,) * (len(extent) - position - 1))

    factor_of = one(*cuts[0])
    for cut in cuts[1:]:
        factor_of = factor_of * one(*cut)
    return factor_of


def setup_inputs(seed: int = 0) -> dict:
    streams_of = jax.random.split(jax.random.key(seed), 3)
    counts = draw_counts(jax.random.fold_in(streams_of[2], 71), 0)
    loadings = jnp.clip(jnp.exp(math.log(0.4) - 2.9957323 * jax.random.uniform(streams_of[1], (NBINS, RANK), jnp.float32) ** block_scale(streams_of[1], (NBINS, RANK), ((0, 32),), -0.2, 0.2)), 0.02, 0.4)
    return dict(counts=counts, loadings=loadings)


def reference(counts, loadings):
    scale = 1.0 / (NBINS ** 0.5)
    columns = jnp.arange(NBINS).astype(jnp.int32)

    def one_block(carry, index):
        start = (index * ROWS_DEV).astype(jnp.int32)
        tile = lax.dynamic_slice_in_dim(counts, start, ROWS_DEV, 0)
        rowblock = lax.dynamic_slice_in_dim(loadings, start, ROWS_DEV, 0)
        rate = jnp.dot(rowblock, loadings.T, precision=lax.Precision.HIGHEST)
        positions = start + jnp.arange(ROWS_DEV).astype(jnp.int32)
        keep = jnp.abs(positions[:, None] - columns[None, :]) >= 2
        ratio = jnp.where(keep, 1.0 - tile / rate, jnp.float32(0.0))
        rowpart = jnp.dot(ratio, loadings, precision=lax.Precision.HIGHEST) * scale
        colpart = jnp.dot(ratio.T, rowblock, precision=lax.Precision.HIGHEST) * scale
        return carry + colpart, rowpart

    start_sum = jnp.zeros((NBINS, RANK), jnp.float32)
    col_grad, pieces = lax.scan(one_block, start_sum, jnp.arange(NBINS // ROWS_DEV).astype(jnp.int32))
    row_grad = pieces.reshape(NBINS, RANK)
    return row_grad, col_grad
```

```python
import functools

import jax
import jax.numpy as jnp
from jax import lax
from jax.experimental import pallas as pl
from jax.experimental.pallas import tpu as pltpu
from jax.sharding import PartitionSpec as P

MESH = pl.DeviceIdType.MESH
NT = (((1,), (1,)), ((), ()))
CHUNK = 256


def broadcast(block, axis, source):
    block = jnp.where(lax.axis_index(axis) == source, block, jnp.zeros_like(block))
    return lax.psum(block, axis)


def plain(counts, loadings):
    rows = counts.shape[0]
    cols = counts.shape[1]
    nrow = lax.axis_size("row")
    ncol = lax.axis_size("col")
    nbins = rows * nrow
    scale = 1.0 / nbins**0.5
    row_index = lax.axis_index("row")
    col_index = lax.axis_index("col")
    colblock = lax.all_gather(loadings, "row", axis=0, tiled=True)
    group = nrow // ncol
    offset = row_index % group * rows
    portion = lax.dynamic_slice_in_dim(colblock, offset, rows, 0)
    rowblock = broadcast(portion, "col", row_index // group)
    rate = jnp.dot(rowblock, colblock.T, precision=lax.Precision.HIGHEST)
    positions = row_index * rows + jnp.arange(rows)
    targets = col_index * cols + jnp.arange(cols)
    keep = jnp.abs(positions[:, None] - targets[None, :]) >= 2
    ratio = jnp.where(keep, 1.0 - counts / rate, jnp.float32(0.0))
    row_grad = lax.psum_scatter(
        jnp.dot(ratio, colblock, precision=lax.Precision.HIGHEST) * scale,
        "col",
        scatter_dimension=0,
        tiled=True,
    )
    col_grad = lax.psum_scatter(
        jnp.einsum("ij,ik->jk", ratio, rowblock, precision=lax.Precision.HIGHEST) * scale,
        "row",
        scatter_dimension=0,
        tiled=True,
    )
    return (row_grad, col_grad)


def split(value):
    high = value.astype(jnp.bfloat16)
    low = (value - high.astype(jnp.float32)).astype(jnp.bfloat16)
    return high, low


def flip(index, bit):
    return index + bit - 2 * bit * (index // bit % 2)


def flips(index, mask):
    bit = 1
    while bit <= mask:
        if mask & bit:
            index = flip(index, bit)
        bit *= 2
    return index


def low_bit(mask):
    return mask & -mask


def kernel(
    nrow, ncol, scale,
    counts_ref, load_ref, row_out, col_out,
    tiles, gathered, rowt, rowcat, rowhl, row_acc, parts, arrived, row_parts, row_arrived,
    tile_sem, ag_send, ag_recv, rs_send, rs_recv, rb_send, rb_recv, rg_send, rg_recv,
):
    rows = counts_ref.shape[0]
    own, rank = load_ref.shape
    me = lax.axis_index("row")
    mycol = lax.axis_index("col")
    bits = []
    bit = 1
    while bit < nrow:
        bits.append(bit)
        bit *= 2

    same = sorted((m for m in range(nrow) if not m & 1), key=lambda m: [m >> k & 1 for k in range(1, len(bits))])
    other = [m | 1 for m in reversed(same)]
    order = same + other

    def tile_copy(m):
        start = pl.multiple_of(flips(me, m) * own, own)
        return pltpu.make_async_copy(counts_ref.at[:, pl.ds(start, own)], tiles.at[m], tile_sem.at[m])

    for m in order:
        tile_copy(m).start()

    barrier = pltpu.get_barrier_semaphore()
    for bit in bits:
        pl.semaphore_signal(barrier, inc=1, device_id=(flip(me, bit), mycol), device_id_type=MESH)
    for d in range(1, ncol):
        pl.semaphore_signal(barrier, inc=1, device_id=(me, (mycol + d) % ncol), device_id_type=MESH)
    for i in range(ncol):
        block = me * ncol + i
        source_row, source_col = block % nrow, block // nrow
        pl.semaphore_signal(
            barrier, inc=1, device_id=(source_row, source_col), device_id_type=MESH
        )

    gathered[0] = load_ref[...].T
    pl.semaphore_wait(barrier, len(bits) + ncol - 1 + ncol)

    mine = mycol * nrow + me
    target, slot = mine // ncol, mine % ncol

    def row_copy(c):
        return pltpu.make_async_remote_copy(
            gathered.at[0], rowt.at[slot], rb_send.at[c], rb_recv.at[slot],
            device_id=(target, c), device_id_type=MESH,
        )

    def local_copy():
        return pltpu.make_async_copy(gathered.at[0], rowt.at[slot], rb_recv.at[slot])

    for c in range(ncol):
        itself = (target == me) & (mycol == c)
        pl.when(itself)(lambda: local_copy().start())
        pl.when(jnp.logical_not(itself))(lambda c=c: row_copy(c).start())

    def gather_copy(r):
        bit = low_bit(r)
        return pltpu.make_async_remote_copy(
            gathered.at[r ^ bit], gathered.at[r], ag_send.at[r], ag_recv.at[r],
            device_id=(flip(me, bit), mycol), device_id_type=MESH,
        )

    def forward(m):
        if m:
            gather_copy(m).wait_recv()
        for bit in reversed(bits):
            if m == 0 or bit < low_bit(m):
                gather_copy(m | bit).start()

    def reduce_copy(m):
        bit = low_bit(m)
        return pltpu.make_async_remote_copy(
            parts.at[m], arrived.at[m], rs_send.at[m], rs_recv.at[m],
            device_id=(flip(me, bit), mycol), device_id_type=MESH,
        )

    def finish(m):
        total = parts[m]
        for bit in bits:
            if m == 0 or bit < low_bit(m):
                reduce_copy(m | bit).wait_recv()
                total += arrived[m | bit]
        if m:
            parts[m] = total
            reduce_copy(m).start()
        return total

    def prepare_rows():
        for i in range(ncol):
            pltpu.make_async_remote_copy(
                gathered.at[0], rowt.at[i], rb_send.at[0], rb_recv.at[i],
                device_id=(me, mycol), device_id_type=MESH,
            ).wait_recv()
        for i in range(ncol):
            high, low = split(rowt[i])
            both = jnp.concatenate([high, low], axis=0)
            rowhl[:, i * own:(i + 1) * own] = both
            wide = jnp.concatenate([both, both], axis=0).astype(jnp.float32)
            rowcat[i * own:(i + 1) * own, :] = wide.T.astype(jnp.bfloat16)

    first_row = me * rows

    def compute(m):
        tile_copy(m).wait()
        high, low = split(gathered[m])
        colcat = jnp.concatenate([high, high, low, low], axis=0)
        colhl = jnp.concatenate([high, low], axis=0)
        first_col = (mycol * nrow + flips(me, m)) * own
        total = None
        for start in range(0, rows, CHUNK):
            span = slice(start, start + CHUNK)
            rate = jnp.dot(rowcat[span, :], colcat, preferred_element_type=jnp.float32)
            guess = pl.reciprocal(rate, approx=True)
            inverse = guess * (2.0 - rate * guess)
            gap = (
                lax.broadcasted_iota(jnp.int32, (CHUNK, own), 0)
                - lax.broadcasted_iota(jnp.int32, (CHUNK, own), 1)
                + (first_row + start - first_col)
            )
            ratio = jnp.where(jnp.abs(gap) >= 2, 1.0 - tiles[m, span, :] * inverse, 0.0)
            high_r, low_r = split(ratio)
            row_part = lax.dot_general(high_r, colhl, NT, preferred_element_type=jnp.float32)
            row_part += lax.dot_general(low_r, colhl, NT, preferred_element_type=jnp.float32)
            if m == order[0]:
                row_acc[span, :] = row_part
            else:
                row_acc[span, :] += row_part
            col_part = jnp.dot(rowhl[:, span], high_r, preferred_element_type=jnp.float32)
            col_part += jnp.dot(rowhl[:, span], low_r, preferred_element_type=jnp.float32)
            total = col_part if total is None else total + col_part
        parts[m] = total[:rank] + total[rank:]
        if m & 1:
            reduce_copy(m).start()

    forwards = list(same)
    ahead = len(same) // 2
    for m in forwards[:ahead]:
        forward(m)
    prepare_rows()
    waiting = forwards[ahead:]
    for m in same:
        if waiting:
            forward(waiting.pop(0))
        compute(m)
    passing = [m for m in reversed(same) if m & 2]
    for k, m in enumerate(other):
        gather_copy(m).wait_recv()
        compute(m)
        if k >= 2 and passing:
            finish(passing.pop(0))
    for m in passing:
        finish(m)

    sums = (row_acc[:, :rank] + row_acc[:, rank:]) * scale
    for c in range(ncol):
        row_parts[c] = sums[c * own:(c + 1) * own].T

    def row_send(d):
        to = (mycol + d) % ncol
        return pltpu.make_async_remote_copy(
            row_parts.at[to], row_arrived.at[d - 1], rg_send.at[d - 1], rg_recv.at[d - 1],
            device_id=(me, to), device_id_type=MESH,
        )

    for d in range(1, ncol):
        row_send(d).start()
    for m in reversed(same):
        if m and not m & 2:
            finish(m)
    row_total = row_parts[mycol]
    for d in range(1, ncol):
        row_send(d).wait_recv()
        row_total += row_arrived[d - 1]
    row_out[...] = row_total.T
    col_out[...] = finish(0).T * scale

    for m in range(1, nrow):
        gather_copy(m).wait_send()
        reduce_copy(m).wait_send()
    for d in range(1, ncol):
        row_send(d).wait_send()
    for c in range(ncol):
        itself = (target == me) & (mycol == c)
        pl.when(jnp.logical_not(itself))(lambda c=c: row_copy(c).wait_send())


def fused(nrow, ncol, counts, loadings):
    rows = counts.shape[0]
    own, rank = loadings.shape
    f32, bf16 = jnp.float32, jnp.bfloat16
    dma = pltpu.SemaphoreType.DMA
    others = max(ncol - 1, 1)
    return pl.pallas_call(
        functools.partial(kernel, nrow, ncol, 1.0 / (rows * nrow) ** 0.5),
        out_shape=(jax.ShapeDtypeStruct((own, rank), f32),) * 2,
        in_specs=[pl.BlockSpec(memory_space=pl.ANY), pl.BlockSpec(memory_space=pltpu.VMEM)],
        out_specs=(pl.BlockSpec(memory_space=pltpu.VMEM),) * 2,
        scratch_shapes=[
            pltpu.VMEM((nrow, rows, own), f32),
            pltpu.VMEM((nrow, rank, own), f32),
            pltpu.VMEM((ncol, rank, own), f32),
            pltpu.VMEM((rows, 4 * rank), bf16),
            pltpu.VMEM((2 * rank, rows), bf16),
            pltpu.VMEM((rows, 2 * rank), f32),
            pltpu.VMEM((nrow, rank, own), f32),
            pltpu.VMEM((nrow, rank, own), f32),
            pltpu.VMEM((ncol, rank, own), f32),
            pltpu.VMEM((others, rank, own), f32),
            dma((nrow,)), dma((nrow,)), dma((nrow,)), dma((nrow,)), dma((nrow,)),
            dma((ncol,)), dma((ncol,)), dma((others,)), dma((others,)),
        ],
        compiler_params=pltpu.CompilerParams(
            collective_id=0, has_side_effects=True, vmem_limit_bytes=60 * 2**20
        ),
    )(counts, loadings)


def solution(mesh):
    nrow, ncol = mesh.shape["row"], mesh.shape["col"]

    def shards(counts, loadings):
        rows = counts.shape[0]
        own, rank = loadings.shape
        fits = nrow >= 4 and nrow & (nrow - 1) == 0 and rows == own * ncol
        fits = fits and own % 128 == 0 and rank % 64 == 0 and rows % CHUNK == 0
        return fused(nrow, ncol, counts, loadings) if fits else plain(counts, loadings)

    placed = (P("row", "col"), P(("col", "row"), None))
    return jax.shard_map(
        shards,
        mesh=mesh,
        in_specs=placed,
        out_specs=(P(("row", "col"), None), P(("col", "row"), None)),
        check_vma=False,
    )
```

```python
import functools

import jax
import jax.numpy as jnp
from jax import lax
from jax.experimental import pallas as pl
from jax.experimental.pallas import tpu as pltpu
from jax.sharding import PartitionSpec as P

MESH = pl.DeviceIdType.MESH
NT = (((1,), (1,)), ((), ()))
CHUNK = 256


def broadcast(block, axis, source):
    block = jnp.where(lax.axis_index(axis) == source, block, jnp.zeros_like(block))
    return lax.psum(block, axis)


def plain(counts, loadings):
    rows = counts.shape[0]
    cols = counts.shape[1]
    nrow = lax.axis_size("row")
    ncol = lax.axis_size("col")
    nbins = rows * nrow
    scale = 1.0 / nbins**0.5
    row_index = lax.axis_index("row")
    col_index = lax.axis_index("col")
    colblock = lax.all_gather(loadings, "row", axis=0, tiled=True)
    group = nrow // ncol
    offset = row_index % group * rows
    portion = lax.dynamic_slice_in_dim(colblock, offset, rows, 0)
    rowblock = broadcast(portion, "col", row_index // group)
    rate = jnp.dot(rowblock, colblock.T, precision=lax.Precision.HIGHEST)
    positions = row_index * rows + jnp.arange(rows)
    targets = col_index * cols + jnp.arange(cols)
    keep = jnp.abs(positions[:, None] - targets[None, :]) >= 2
    ratio = jnp.where(keep, 1.0 - counts / rate, jnp.float32(0.0))
    row_grad = lax.psum_scatter(
        jnp.dot(ratio, colblock, precision=lax.Precision.HIGHEST) * scale,
        "col",
        scatter_dimension=0,
        tiled=True,
    )
    col_grad = lax.psum_scatter(
        jnp.einsum("ij,ik->jk", ratio, rowblock, precision=lax.Precision.HIGHEST) * scale,
        "row",
        scatter_dimension=0,
        tiled=True,
    )
    return (row_grad, col_grad)


def split(value):
    high = value.astype(jnp.bfloat16)
    low = (value - high.astype(jnp.float32)).astype(jnp.bfloat16)
    return high, low


def flip(index, bit):
    return index + bit - 2 * bit * (index // bit % 2)


def flips(index, mask):
    bit = 1
    while bit <= mask:
        if mask & bit:
            index = flip(index, bit)
        bit *= 2
    return index


def low_bit(mask):
    return mask & -mask


def kernel(
    nrow, ncol, scale,
    counts_ref, load_ref, row_out, col_out,
    tiles, gathered, rowt, rowcat, rowhl, row_acc, parts, arrived, row_parts, row_arrived,
    load_sem, tile_sem, ag_send, ag_recv, rs_send, rs_recv, rb_send, rb_recv, rg_send, rg_recv,
):
    rows = counts_ref.shape[0]
    rank, own = load_ref.shape
    me = lax.axis_index("row")
    mycol = lax.axis_index("col")
    bits = []
    bit = 1
    while bit < nrow:
        bits.append(bit)
        bit *= 2

    same = sorted((m for m in range(nrow) if not m & 1), key=lambda m: [m >> k & 1 for k in range(1, len(bits))])
    other = [m | 1 for m in reversed(same)]
    order = same + other

    def tile_copy(m):
        start = pl.multiple_of(flips(me, m) * own, own)
        return pltpu.make_async_copy(counts_ref.at[:, pl.ds(start, own)], tiles.at[m], tile_sem.at[m])

    fetch = pltpu.make_async_copy(load_ref, gathered.at[0], load_sem)
    fetch.start()

    barrier = pltpu.get_barrier_semaphore()
    for bit in bits:
        pl.semaphore_signal(barrier, inc=1, device_id=(flip(me, bit), mycol), device_id_type=MESH)
    for d in range(1, ncol):
        pl.semaphore_signal(barrier, inc=1, device_id=(me, (mycol + d) % ncol), device_id_type=MESH)
    for i in range(ncol):
        block = me * ncol + i
        source_row, source_col = block % nrow, block // nrow
        pl.semaphore_signal(
            barrier, inc=1, device_id=(source_row, source_col), device_id_type=MESH
        )

    for m in order:
        tile_copy(m).start()
    fetch.wait()
    pl.semaphore_wait(barrier, len(bits) + ncol - 1 + ncol)

    mine = mycol * nrow + me
    target, slot = mine // ncol, mine % ncol

    def row_copy(c):
        return pltpu.make_async_remote_copy(
            gathered.at[0], rowt.at[slot], rb_send.at[c], rb_recv.at[slot],
            device_id=(target, c), device_id_type=MESH,
        )

    def local_copy():
        return pltpu.make_async_copy(gathered.at[0], rowt.at[slot], rb_recv.at[slot])

    for c in range(ncol):
        itself = (target == me) & (mycol == c)
        pl.when(itself)(lambda: local_copy().start())
        pl.when(jnp.logical_not(itself))(lambda c=c: row_copy(c).start())

    def gather_copy(r):
        bit = low_bit(r)
        return pltpu.make_async_remote_copy(
            gathered.at[r ^ bit], gathered.at[r], ag_send.at[r], ag_recv.at[r],
            device_id=(flip(me, bit), mycol), device_id_type=MESH,
        )

    def forward(m):
        if m:
            gather_copy(m).wait_recv()
        for bit in reversed(bits):
            if m == 0 or bit < low_bit(m):
                gather_copy(m | bit).start()

    def reduce_copy(m):
        bit = low_bit(m)
        return pltpu.make_async_remote_copy(
            parts.at[m], arrived.at[m], rs_send.at[m], rs_recv.at[m],
            device_id=(flip(me, bit), mycol), device_id_type=MESH,
        )

    def finish(m):
        total = parts[m]
        for bit in bits:
            if m == 0 or bit < low_bit(m):
                reduce_copy(m | bit).wait_recv()
                total += arrived[m | bit]
        if m:
            parts[m] = total
            reduce_copy(m).start()
        return total

    def prepare_rows():
        for i in range(ncol):
            pltpu.make_async_remote_copy(
                gathered.at[0], rowt.at[i], rb_send.at[0], rb_recv.at[i],
                device_id=(me, mycol), device_id_type=MESH,
            ).wait_recv()
        for i in range(ncol):
            high, low = split(rowt[i])
            both = jnp.concatenate([high, low], axis=0)
            rowhl[:, i * own:(i + 1) * own] = both
            wide = jnp.concatenate([both, both], axis=0).astype(jnp.float32)
            rowcat[i * own:(i + 1) * own, :] = wide.T.astype(jnp.bfloat16)

    first_row = me * rows

    def compute(m):
        tile_copy(m).wait()
        high, low = split(gathered[m])
        colcat = jnp.concatenate([high, high, low, low], axis=0)
        colhl = jnp.concatenate([high, low], axis=0)
        first_col = (mycol * nrow + flips(me, m)) * own
        total = None
        for start in range(0, rows, CHUNK):
            span = slice(start, start + CHUNK)
            rate = jnp.dot(rowcat[span, :], colcat, preferred_element_type=jnp.float32)
            guess = pl.reciprocal(rate, approx=True)
            inverse = guess * (2.0 - rate * guess)
            gap = (
                lax.broadcasted_iota(jnp.int32, (CHUNK, own), 0)
                - lax.broadcasted_iota(jnp.int32, (CHUNK, own), 1)
                + (first_row + start - first_col)
            )
            ratio = jnp.where(jnp.abs(gap) >= 2, 1.0 - tiles[m, span, :] * inverse, 0.0)
            high_r, low_r = split(ratio)
            row_part = lax.dot_general(high_r, colhl, NT, preferred_element_type=jnp.float32)
            row_part += lax.dot_general(low_r, colhl, NT, preferred_element_type=jnp.float32)
            if m == order[0]:
                row_acc[span, :] = row_part
            else:
                row_acc[span, :] += row_part
            col_part = jnp.dot(rowhl[:, span], high_r, preferred_element_type=jnp.float32)
            col_part += jnp.dot(rowhl[:, span], low_r, preferred_element_type=jnp.float32)
            total = col_part if total is None else total + col_part
        parts[m] = total[:rank] + total[rank:]
        if m & 1:
            reduce_copy(m).start()

    forwards = list(same)
    ahead = len(same) // 2
    for m in forwards[:ahead]:
        forward(m)
    prepare_rows()
    waiting = forwards[ahead:]
    for m in same:
        if waiting:
            forward(waiting.pop(0))
        compute(m)
    passing = [m for m in reversed(same) if m & 2]
    for k, m in enumerate(other):
        gather_copy(m).wait_recv()
        compute(m)
        if k >= 2 and passing:
            finish(passing.pop(0))
    for m in passing:
        finish(m)

    sums = (row_acc[:, :rank] + row_acc[:, rank:]) * scale
    for c in range(ncol):
        row_parts[c] = sums[c * own:(c + 1) * own].T

    def row_send(d):
        to = (mycol + d) % ncol
        return pltpu.make_async_remote_copy(
            row_parts.at[to], row_arrived.at[d - 1], rg_send.at[d - 1], rg_recv.at[d - 1],
            device_id=(me, to), device_id_type=MESH,
        )

    for d in range(1, ncol):
        row_send(d).start()
    for m in reversed(same):
        if m and not m & 2:
            finish(m)
    row_total = row_parts[mycol]
    for d in range(1, ncol):
        row_send(d).wait_recv()
        row_total += row_arrived[d - 1]
    row_out[...] = row_total
    col_out[...] = finish(0) * scale

    for m in range(1, nrow):
        gather_copy(m).wait_send()
        reduce_copy(m).wait_send()
    for d in range(1, ncol):
        row_send(d).wait_send()
    for c in range(ncol):
        itself = (target == me) & (mycol == c)
        pl.when(jnp.logical_not(itself))(lambda c=c: row_copy(c).wait_send())


def fused(nrow, ncol, counts, loadings):
    rows = counts.shape[0]
    own, rank = loadings.shape
    f32, bf16 = jnp.float32, jnp.bfloat16
    dma = pltpu.SemaphoreType.DMA
    others = max(ncol - 1, 1)
    row_grad, col_grad = pl.pallas_call(
        functools.partial(kernel, nrow, ncol, 1.0 / (rows * nrow) ** 0.5),
        out_shape=(jax.ShapeDtypeStruct((rank, own), f32),) * 2,
        in_specs=[pl.BlockSpec(memory_space=pl.ANY)] * 2,
        out_specs=(pl.BlockSpec(memory_space=pltpu.VMEM),) * 2,
        scratch_shapes=[
            pltpu.VMEM((nrow, rows, own), f32),
            pltpu.VMEM((nrow, rank, own), f32),
            pltpu.VMEM((ncol, rank, own), f32),
            pltpu.VMEM((rows, 4 * rank), bf16),
            pltpu.VMEM((2 * rank, rows), bf16),
            pltpu.VMEM((rows, 2 * rank), f32),
            pltpu.VMEM((nrow, rank, own), f32),
            pltpu.VMEM((nrow, rank, own), f32),
            pltpu.VMEM((ncol, rank, own), f32),
            pltpu.VMEM((others, rank, own), f32),
            dma, dma((nrow,)), dma((nrow,)), dma((nrow,)), dma((nrow,)), dma((nrow,)),
            dma((ncol,)), dma((ncol,)), dma((others,)), dma((others,)),
        ],
        compiler_params=pltpu.CompilerParams(
            collective_id=0, has_side_effects=True, vmem_limit_bytes=60 * 2**20
        ),
    )(counts, loadings.T)
    return row_grad.T, col_grad.T


def solution(mesh):
    nrow, ncol = mesh.shape["row"], mesh.shape["col"]

    def shards(counts, loadings):
        rows = counts.shape[0]
        own, rank = loadings.shape
        fits = nrow >= 4 and nrow & (nrow - 1) == 0 and rows == own * ncol
        fits = fits and own % 128 == 0 and rank % 64 == 0 and rows % CHUNK == 0
        return fused(nrow, ncol, counts, loadings) if fits else plain(counts, loadings)

    placed = (P("row", "col"), P(("col", "row"), None))
    return jax.shard_map(
        shards,
        mesh=mesh,
        in_specs=placed,
        out_specs=(P(("row", "col"), None), P(("col", "row"), None)),
        check_vma=False,
    )
```

```python
import functools

import jax
import jax.numpy as jnp
from jax import lax
from jax.experimental import pallas as pl
from jax.experimental.pallas import tpu as pltpu
from jax.sharding import PartitionSpec as P

MESH = pl.DeviceIdType.MESH
NT = (((1,), (1,)), ((), ()))
CHUNK = 256


def broadcast(block, axis, source):
    block = jnp.where(lax.axis_index(axis) == source, block, jnp.zeros_like(block))
    return lax.psum(block, axis)


def plain(counts, loadings):
    rows = counts.shape[0]
    cols = counts.shape[1]
    nrow = lax.axis_size("row")
    ncol = lax.axis_size("col")
    nbins = rows * nrow
    scale = 1.0 / nbins**0.5
    row_index = lax.axis_index("row")
    col_index = lax.axis_index("col")
    colblock = lax.all_gather(loadings, "row", axis=0, tiled=True)
    group = nrow // ncol
    offset = row_index % group * rows
    portion = lax.dynamic_slice_in_dim(colblock, offset, rows, 0)
    rowblock = broadcast(portion, "col", row_index // group)
    rate = jnp.dot(rowblock, colblock.T, precision=lax.Precision.HIGHEST)
    positions = row_index * rows + jnp.arange(rows)
    targets = col_index * cols + jnp.arange(cols)
    keep = jnp.abs(positions[:, None] - targets[None, :]) >= 2
    ratio = jnp.where(keep, 1.0 - counts / rate, jnp.float32(0.0))
    row_grad = lax.psum_scatter(
        jnp.dot(ratio, colblock, precision=lax.Precision.HIGHEST) * scale,
        "col",
        scatter_dimension=0,
        tiled=True,
    )
    col_grad = lax.psum_scatter(
        jnp.einsum("ij,ik->jk", ratio, rowblock, precision=lax.Precision.HIGHEST) * scale,
        "row",
        scatter_dimension=0,
        tiled=True,
    )
    return (row_grad, col_grad)


def split(value):
    high = value.astype(jnp.bfloat16)
    low = (value - high.astype(jnp.float32)).astype(jnp.bfloat16)
    return high, low


def flip(index, bit):
    return index + bit - 2 * bit * (index // bit % 2)


def flips(index, mask):
    bit = 1
    while bit <= mask:
        if mask & bit:
            index = flip(index, bit)
        bit *= 2
    return index


def low_bit(mask):
    return mask & -mask


def kernel(
    nrow, ncol, scale,
    counts_ref, load_ref, row_out, col_out,
    tiles, gathered, rowt, rowcat, rowhl, row_acc, parts, arrived, row_parts, row_arrived,
    load_sem, tile_sem, ag_send, ag_recv, rs_send, rs_recv, rb_send, rb_recv, rg_send, rg_recv,
):
    rows = counts_ref.shape[0]
    rank, own = load_ref.shape
    me = lax.axis_index("row")
    mycol = lax.axis_index("col")
    bits = []
    bit = 1
    while bit < nrow:
        bits.append(bit)
        bit *= 2

    same = sorted((m for m in range(nrow) if not m & 1), key=lambda m: [m >> k & 1 for k in range(1, len(bits))])
    other = [m | 1 for m in reversed(same)]
    order = same + other

    def tile_copy(m):
        start = pl.multiple_of(flips(me, m) * own, own)
        return pltpu.make_async_copy(counts_ref.at[:, pl.ds(start, own)], tiles.at[m], tile_sem.at[m])

    fetch = pltpu.make_async_copy(load_ref, gathered.at[0], load_sem)
    fetch.start()

    barrier = pltpu.get_barrier_semaphore()
    for bit in bits:
        pl.semaphore_signal(barrier, inc=1, device_id=(flip(me, bit), mycol), device_id_type=MESH)
    for d in range(1, ncol):
        pl.semaphore_signal(barrier, inc=1, device_id=(me, (mycol + d) % ncol), device_id_type=MESH)
    for i in range(ncol):
        block = me * ncol + i
        source_row, source_col = block % nrow, block // nrow
        pl.semaphore_signal(
            barrier, inc=1, device_id=(source_row, source_col), device_id_type=MESH
        )

    for m in order:
        tile_copy(m).start()
    fetch.wait()
    pl.semaphore_wait(barrier, len(bits) + ncol - 1 + ncol)

    mine = mycol * nrow + me
    target, slot = mine // ncol, mine % ncol

    def row_copy(c):
        return pltpu.make_async_remote_copy(
            gathered.at[0], rowt.at[slot], rb_send.at[c], rb_recv.at[slot],
            device_id=(target, c), device_id_type=MESH,
        )

    def local_copy():
        return pltpu.make_async_copy(gathered.at[0], rowt.at[slot], rb_recv.at[slot])

    def start_rows():
        for c in range(ncol):
            itself = (target == me) & (mycol == c)
            pl.when(itself)(lambda: local_copy().start())
            pl.when(jnp.logical_not(itself))(lambda c=c: row_copy(c).start())

    def gather_copy(r):
        bit = low_bit(r)
        return pltpu.make_async_remote_copy(
            gathered.at[r ^ bit], gathered.at[r], ag_send.at[r], ag_recv.at[r],
            device_id=(flip(me, bit), mycol), device_id_type=MESH,
        )

    def forward(m):
        if m:
            gather_copy(m).wait_recv()
        for bit in reversed(bits):
            if m == 0 or bit < low_bit(m):
                gather_copy(m | bit).start()

    def reduce_copy(m):
        bit = low_bit(m)
        return pltpu.make_async_remote_copy(
            parts.at[m], arrived.at[m], rs_send.at[m], rs_recv.at[m],
            device_id=(flip(me, bit), mycol), device_id_type=MESH,
        )

    def finish(m):
        total = parts[m]
        for bit in bits:
            if m == 0 or bit < low_bit(m):
                reduce_copy(m | bit).wait_recv()
                total += arrived[m | bit]
        if m:
            parts[m] = total
            reduce_copy(m).start()
        return total

    def prepare_rows():
        for i in range(ncol):
            pltpu.make_async_remote_copy(
                gathered.at[0], rowt.at[i], rb_send.at[0], rb_recv.at[i],
                device_id=(me, mycol), device_id_type=MESH,
            ).wait_recv()
        for i in range(ncol):
            high, low = split(rowt[i])
            both = jnp.concatenate([high, low], axis=0)
            rowhl[:, i * own:(i + 1) * own] = both
            wide = jnp.concatenate([both, both], axis=0).astype(jnp.float32)
            rowcat[i * own:(i + 1) * own, :] = wide.T.astype(jnp.bfloat16)

    first_row = me * rows

    def compute(m):
        tile_copy(m).wait()
        high, low = split(gathered[m])
        colcat = jnp.concatenate([high, high, low, low], axis=0)
        colhl = jnp.concatenate([high, low], axis=0)
        first_col = (mycol * nrow + flips(me, m)) * own
        total = None
        for start in range(0, rows, CHUNK):
            span = slice(start, start + CHUNK)
            rate = jnp.dot(rowcat[span, :], colcat, preferred_element_type=jnp.float32)
            guess = pl.reciprocal(rate, approx=True)
            inverse = guess * (2.0 - rate * guess)
            gap = (
                lax.broadcasted_iota(jnp.int32, (CHUNK, own), 0)
                - lax.broadcasted_iota(jnp.int32, (CHUNK, own), 1)
                + (first_row + start - first_col)
            )
            ratio = jnp.where(jnp.abs(gap) >= 2, 1.0 - tiles[m, span, :] * inverse, 0.0)
            high_r, low_r = split(ratio)
            row_part = lax.dot_general(high_r, colhl, NT, preferred_element_type=jnp.float32)
            row_part += lax.dot_general(low_r, colhl, NT, preferred_element_type=jnp.float32)
            if m == order[0]:
                row_acc[span, :] = row_part
            else:
                row_acc[span, :] += row_part
            col_part = jnp.dot(rowhl[:, span], high_r, preferred_element_type=jnp.float32)
            col_part += jnp.dot(rowhl[:, span], low_r, preferred_element_type=jnp.float32)
            total = col_part if total is None else total + col_part
        parts[m] = total[:rank] + total[rank:]
        if m & 1:
            reduce_copy(m).start()

    forwards = list(same)
    ahead = max(len(same) * 3 // 8, 1)
    for m in forwards[:ahead]:
        forward(m)
        if m == 0:
            start_rows()
    prepare_rows()
    waiting = forwards[ahead:]
    for m in same:
        if waiting:
            forward(waiting.pop(0))
        compute(m)
    passing = [m for m in reversed(same) if m & 2]
    for k, m in enumerate(other):
        gather_copy(m).wait_recv()
        compute(m)
        if k >= 2 and passing:
            finish(passing.pop(0))
    for m in passing:
        finish(m)

    sums = (row_acc[:, :rank] + row_acc[:, rank:]) * scale
    for c in range(ncol):
        row_parts[c] = sums[c * own:(c + 1) * own].T

    def row_send(d):
        to = (mycol + d) % ncol
        return pltpu.make_async_remote_copy(
            row_parts.at[to], row_arrived.at[d - 1], rg_send.at[d - 1], rg_recv.at[d - 1],
            device_id=(me, to), device_id_type=MESH,
        )

    for d in range(1, ncol):
        row_send(d).start()
    for m in reversed(same):
        if m and not m & 2:
            finish(m)
    row_total = row_parts[mycol]
    for d in range(1, ncol):
        row_send(d).wait_recv()
        row_total += row_arrived[d - 1]
    row_out[...] = row_total
    col_out[...] = finish(0) * scale

    for m in range(1, nrow):
        gather_copy(m).wait_send()
        reduce_copy(m).wait_send()
    for d in range(1, ncol):
        row_send(d).wait_send()
    for c in range(ncol):
        itself = (target == me) & (mycol == c)
        pl.when(jnp.logical_not(itself))(lambda c=c: row_copy(c).wait_send())


def fused(nrow, ncol, counts, loadings):
    rows = counts.shape[0]
    own, rank = loadings.shape
    f32, bf16 = jnp.float32, jnp.bfloat16
    dma = pltpu.SemaphoreType.DMA
    others = max(ncol - 1, 1)
    row_grad, col_grad = pl.pallas_call(
        functools.partial(kernel, nrow, ncol, 1.0 / (rows * nrow) ** 0.5),
        out_shape=(jax.ShapeDtypeStruct((rank, own), f32),) * 2,
        in_specs=[pl.BlockSpec(memory_space=pl.ANY)] * 2,
        out_specs=(pl.BlockSpec(memory_space=pltpu.VMEM),) * 2,
        scratch_shapes=[
            pltpu.VMEM((nrow, rows, own), f32),
            pltpu.VMEM((nrow, rank, own), f32),
            pltpu.VMEM((ncol, rank, own), f32),
            pltpu.VMEM((rows, 4 * rank), bf16),
            pltpu.VMEM((2 * rank, rows), bf16),
            pltpu.VMEM((rows, 2 * rank), f32),
            pltpu.VMEM((nrow, rank, own), f32),
            pltpu.VMEM((nrow, rank, own), f32),
            pltpu.VMEM((ncol, rank, own), f32),
            pltpu.VMEM((others, rank, own), f32),
            dma, dma((nrow,)), dma((nrow,)), dma((nrow,)), dma((nrow,)), dma((nrow,)),
            dma((ncol,)), dma((ncol,)), dma((others,)), dma((others,)),
        ],
        compiler_params=pltpu.CompilerParams(
            collective_id=0, has_side_effects=True, vmem_limit_bytes=60 * 2**20
        ),
    )(counts, loadings.T)
    return row_grad.T, col_grad.T


def solution(mesh):
    nrow, ncol = mesh.shape["row"], mesh.shape["col"]

    def shards(counts, loadings):
        rows = counts.shape[0]
        own, rank = loadings.shape
        fits = nrow >= 4 and nrow & (nrow - 1) == 0 and rows == own * ncol
        fits = fits and own % 128 == 0 and rank % 64 == 0 and rows % CHUNK == 0
        return fused(nrow, ncol, counts, loadings) if fits else plain(counts, loadings)

    placed = (P("row", "col"), P(("col", "row"), None))
    return jax.shard_map(
        shards,
        mesh=mesh,
        in_specs=placed,
        out_specs=(P(("row", "col"), None), P(("col", "row"), None)),
        check_vma=False,
    )
```
